32 devices in a mesh: groups: 2 (over y), width: 4 (over z), hidden: 4 (over x, core).
Axes of the slice: x: 2, y: 2, z: 4, core: 2. Of those that a mesh axis runs over, the one named last changes fastest.
Arguments:
- inputs: bfloat16 [2, 16, 8192], P(None, 'groups', 'width'), parts along dimension 1, may hold values from -6 to 6
- attn_gain: float32 [8192], P('width'), may hold values from 0.5 to 2
- w_query: bfloat16 [8192, 8192], P('width', 'hidden'), may hold values from -0.0625 to 0.0625
- w_key: bfloat16 [8192, 1024], P('width', 'hidden'), may hold values from -0.0625 to 0.0625
- w_value: bfloat16 [8192, 1024], P('width', 'hidden'), may hold values from -0.0625 to 0.0625
- w_out: bfloat16 [8192, 8192], P('hidden', 'width'), may hold values from -0.0625 to 0.0625
- ffn_gain: float32 [8192], P('width'), may hold values from 0.5 to 2
- w_gate: bfloat16 [8192, 14336], P('width', 'hidden'), may hold values from -0.0625 to 0.0625
- w_up: bfloat16 [8192, 14336], P('width', 'hidden'), may hold values from -0.0625 to 0.0625
- w_down: bfloat16 [14336, 8192], P('hidden', 'width'), may hold values from -0.046875 to 0.046875
- key_cache: bfloat16 [16, 8, 2048, 128], P(('groups', 'width'), 'hidden'), parts along dimension 0
- value_cache: bfloat16 [16, 8, 2048, 128], P(('groups', 'width'), 'hidden'), parts along dimension 0, may hold values from -6 to 6
- lengths: int32 [16], P(('groups', 'width')), parts along dimension 0, may hold values from 1 to 2046, as said below
- positions: int32 [16], P(('groups', 'width')), parts along dimension 0, may hold values from 0 to 8191
Outputs:
- outputs: bfloat16 [2, 16, 8192], P(None, 'groups', 'width'), parts along dimension 1
The draws below stay inside these ranges and needn't reach their ends.
There are 2 independent parts, one for each index of `groups`. The reference program is written for one: setup_inputs(seed, part) draws one part's arguments, and reference() takes and returns one part's arrays. A program takes and returns all parts, laid end to end along the dimension named above; an argument that names none is the same for every part. Nothing has to cross between parts.
Inputs may be any that keep to these rules, and one draw needn't show every extreme that they name: `lengths`: some request has exactly 2046 filled slots and some has exactly one.
All inputs are finite; a program needn't handle non-finite values.
Results may differ from the reference program's by a relative error of at most 0.0082.
Values may be sent and summed in bfloat16 or wider, within the bound.
A program may use at most 128 MiB of HBM per device.

```python
import math
import jax
import jax.numpy as jnp
from jax import lax

D = 8192
HQ = 64
KVH = 8
HD = 128
FF = 14336
STEPS = 2
CACHE = 2048
REQ = 8


def draw_key_cache(key, part):
    base = jnp.clip(jax.random.normal(key, (REQ, KVH, CACHE, HD), jnp.float32), -6.0, 6.0)
    return base.astype(jnp.bfloat16)


def draw_lengths(key, part):
    first_key = jax.random.fold_in(key, 11)
    second_key = jax.random.fold_in(key, 12)
    third_key = jax.random.fold_in(key, 13)
    filled = jax.random.randint(first_key, (REQ,), 1, CACHE - STEPS + 1, dtype=jnp.int32)
    longest = jax.random.randint(second_key, (), 0, REQ, dtype=jnp.int32)
    shortest = (longest + jax.random.randint(third_key, (), 1, REQ, dtype=jnp.int32)) % REQ
    filled = filled.at[longest].set(CACHE - STEPS)
    filled = filled.at[shortest].set(1)
    return filled


def plant(result, stream_key, smallest, largest):
    spot = [jax.random.randint(jax.random.fold_in(stream_key, axis), (), 0, length) for axis, length in enumerate(result.shape)]
    main_axis = result.shape.index(max(result.shape))
    beside = spot[:main_axis] + [(spot[main_axis] + 1) % result.shape[main_axis]] + spot[main_axis + 1:]
    return result.at[tuple(spot)].set(smallest).at[tuple(beside)].set(largest)


def levels(stream_key, shape, pieces, low, top_value):
    factor_of = 1.0
    for axis_at, blocks in pieces:
        heights = jax.random.uniform(jax.random.fold_in(jax.random.fold_in(stream_key, 6), axis_at), (blocks,), jnp.float32, low / len(pieces), top_value / len(pieces))
        factor_of = factor_of * jnp.repeat(jnp.exp(heights), shape[axis_at] // blocks).reshape((-1,) + (1,) * (len(shape) - 1 - axis_at))
    return factor_of


def noise(own_key, dims, spread, most, shards=(), kind=jnp.bfloat16):
    array = jax.random.normal(own_key, dims, jnp.float32) * spread
    if len(shards) > 0:
        array = levels(own_key, dims, shards, -0.22, 0.18) * array
    return jnp.clip(array, min=-most, max=most).astype(kind)


def setup_inputs(seed: int = 0, part: int = 0) -> dict:
    seeds = jax.random.split(jax.random.key(seed), 15)
    part_keys = jax.random.split(jax.random.fold_in(seeds[14], part), 15)
    inputs = noise(part_keys[0], (STEPS, REQ, D), 1.0, 6.0, ((2, 4),))
    attn_gain = jnp.clip(jnp.exp(math.log(2.0) - 1.3862944 * jax.random.uniform(seeds[1], (D,), jnp.float32) ** levels(seeds[1], (D,), ((0, 4),), -0.2, 0.2)), 0.5, 2.0)
    w_query = noise(seeds[2], (D, HQ * HD), D ** -0.5, 0.0625, ((0, 4), (1, 4)))
    w_key = noise(seeds[3], (D, KVH * HD), D ** -0.5, 0.0625, ((0, 4), (1, 4)))
    w_value = noise(seeds[4], (D, KVH * HD), D ** -0.5, 0.0625, ((0, 4), (1, 4)))
    w_out = noise(seeds[5], (HQ * HD, D), (HQ * HD) ** -0.5, 0.0625, ((0, 4), (1, 4)))
    ffn_gain = jnp.clip(jnp.exp(math.log(2.0) - 1.3862944 * jax.random.uniform(seeds[6], (D,), jnp.float32) ** levels(seeds[6], (D,), ((0, 4),), -0.2, 0.2)), 0.5, 2.0)
    w_gate = noise(seeds[7], (D, FF), D ** -0.5, 0.0625, ((0, 4), (1, 4)))
    w_up = noise(seeds[8], (D, FF), D ** -0.5, 0.0625, ((0, 4), (1, 4)))
    w_down = noise(seeds[9], (FF, D), FF ** -0.5, 0.046875, ((0, 4), (1, 4)))
    key_cache = draw_key_cache(jax.random.fold_in(jax.random.fold_in(seeds[14], part), 71), part)
    value_cache = noise(part_keys[11], (REQ, KVH, CACHE, HD), 1.0, 6.0, ((0, 4), (1, 4)))
    lengths = draw_lengths(jax.random.fold_in(jax.random.fold_in(seeds[14], part), 71), part)
    positions = plant(jax.random.randint(part_keys[13], (REQ,), 0, 8192), jax.random.fold_in(part_keys[13], 1), 0, 8191).astype(jnp.int32)
    return dict(inputs=inputs, attn_gain=attn_gain, w_query=w_query, w_key=w_key, w_value=w_value, w_out=w_out, ffn_gain=ffn_gain, w_gate=w_gate, w_up=w_up, w_down=w_down, key_cache=key_cache, value_cache=value_cache, lengths=lengths, positions=positions)


def rotary(vectors, places):
    half_dim = vectors.shape[-1] // 2
    freqs = 500000.0 ** (-(jnp.arange(half_dim, dtype=jnp.float32) * 2.0 / vectors.shape[-1]))
    angles = places.astype(jnp.float32)[:, None, None] * freqs
    cosine = jnp.cos(angles)
    sine_vals = jnp.sin(angles)
    first_half = vectors[..., :half_dim]
    second_half = vectors[..., half_dim:]
    return jnp.concatenate([first_half * cosine - second_half * sine_vals, second_half * cosine + first_half * sine_vals], axis=-1)

def rms_scale(values, gain):
    mean_square = lax.optimization_barrier(jnp.mean(values * values, axis=-1, keepdims=True))
    return (values * lax.rsqrt(mean_square + 1e-05) * gain).astype(jnp.bfloat16)

def attention(queries, keys, values, slots):
    rows = queries.shape[0]
    kv_count = keys.shape[1]
    grouped = queries.reshape(rows, kv_count, -1, HD).astype(jnp.float32)
    scores = jnp.einsum('rkgd,rkcd->rkgc', grouped, keys.astype(jnp.float32)) / math.sqrt(HD)
    visible = jnp.arange(keys.shape[2], dtype=jnp.int32)[None, None, None, :] <= slots[:, None, None, None]
    scores = jnp.where(visible, scores, -1e+30)
    highest = lax.optimization_barrier(jnp.max(scores, axis=-1, keepdims=True))
    weights = jnp.where(visible, jnp.exp(scores - highest), 0.0)
    probs = (weights / lax.optimization_barrier(jnp.sum(weights, axis=-1, keepdims=True))).astype(jnp.bfloat16)
    mixed = jnp.einsum('rkgc,rkcd->rkgd', probs.astype(jnp.float32), values.astype(jnp.float32))
    return mixed.astype(jnp.bfloat16).reshape(rows, -1)

def reference(inputs, attn_gain, w_query, w_key, w_value, w_out, ffn_gain, w_gate, w_up, w_down, key_cache, value_cache, lengths, positions):
    keys = key_cache
    values = value_cache
    request_ids = jnp.arange(REQ, dtype=jnp.int32)
    results = []
    for step_index in range(STEPS):
        current = inputs[step_index].astype(jnp.float32)
        normed = rms_scale(current, attn_gain)
        queries = jnp.dot(normed, w_query, preferred_element_type=jnp.float32).reshape(REQ, HQ, HD)
        new_keys = jnp.dot(normed, w_key, preferred_element_type=jnp.float32).reshape(REQ, KVH, HD)
        new_values = jnp.dot(normed, w_value, preferred_element_type=jnp.float32).reshape(REQ, KVH, HD)
        places = positions + step_index
        queries = rotary(queries, places).astype(jnp.bfloat16)
        new_keys = rotary(new_keys, places).astype(jnp.bfloat16)
        new_values = new_values.astype(jnp.bfloat16)
        slots = (lengths + step_index).astype(jnp.int32)
        keys = keys.at[request_ids, :, slots].set(new_keys)
        values = values.at[request_ids, :, slots].set(new_values)
        mixed = attention(queries, keys, values, slots)
        residual = current + jnp.dot(mixed, w_out, preferred_element_type=jnp.float32)
        ffn_in = rms_scale(residual, ffn_gain)
        gate = jnp.dot(ffn_in, w_gate, preferred_element_type=jnp.float32)
        up_part = jnp.dot(ffn_in, w_up, preferred_element_type=jnp.float32)
        activated = (jax.nn.silu(gate) * up_part).astype(jnp.bfloat16)
        results.append((residual + jnp.dot(activated, w_down, preferred_element_type=jnp.float32)).astype(jnp.bfloat16))
    return jnp.stack(results)
```

```python
import functools
import math

import jax
import jax.numpy as jnp
import numpy as np
from jax import lax
from jax.experimental import pallas as pl
from jax.experimental.pallas import tpu as pltpu
from jax.sharding import PartitionSpec as P

HD = 128


def rotary(vectors, places):
    half_dim = vectors.shape[-1] // 2
    freqs = 500000.0 ** (-(jnp.arange(half_dim, dtype=jnp.float32) * 2.0 / vectors.shape[-1]))
    angles = places.astype(jnp.float32)[:, None, None] * freqs
    cosine = jnp.cos(angles)
    sine_vals = jnp.sin(angles)
    first_half = vectors[..., :half_dim]
    second_half = vectors[..., half_dim:]
    return jnp.concatenate(
        [
            first_half * cosine - second_half * sine_vals,
            second_half * cosine + first_half * sine_vals,
        ],
        axis=-1,
    )


def attention(queries, keys, values, new_keys, new_values, lengths):
    rows, steps = queries.shape[:2]
    kv_count = keys.shape[1]
    grouped = queries.reshape(rows, steps, kv_count, -1, HD)
    scale = 1.0 / math.sqrt(HD)
    old = jnp.einsum("rskgd,rkcd->rksgc", grouped, keys, preferred_element_type=jnp.float32) * scale
    new = (
        jnp.einsum("rskgd,rtkd->rksgt", grouped, new_keys, preferred_element_type=jnp.float32)
        * scale
    )
    seen = jnp.arange(keys.shape[2], dtype=jnp.int32) < lengths[:, None]
    seen = seen[:, None, None, None, :]
    order = jnp.arange(steps)[None, :] <= jnp.arange(steps)[:, None]
    order = order[None, None, :, None, :]
    old = jnp.where(seen, old, -1e30)
    new = jnp.where(order, new, -1e30)
    highest = jnp.maximum(jnp.max(old, axis=-1, keepdims=True), jnp.max(new, axis=-1, keepdims=True))
    old = jnp.where(seen, jnp.exp(old - highest), 0.0)
    new = jnp.where(order, jnp.exp(new - highest), 0.0)
    total = jnp.sum(old, axis=-1, keepdims=True) + jnp.sum(new, axis=-1, keepdims=True)
    old = (old / total).astype(jnp.bfloat16)
    new = (new / total).astype(jnp.bfloat16)
    mixed = jnp.einsum("rksgc,rkcd->rskgd", old, values, preferred_element_type=jnp.float32)
    mixed += jnp.einsum("rksgt,rtkd->rskgd", new, new_values, preferred_element_type=jnp.float32)
    return mixed.astype(jnp.bfloat16).reshape(rows, steps, -1)


def plain(
    inputs,
    attn_gain,
    w_query,
    w_key,
    w_value,
    w_out,
    ffn_gain,
    w_gate,
    w_up,
    w_down,
    key_cache,
    value_cache,
    lengths,
    positions,
):
    local_rows = key_cache.shape[0]
    steps, requests, depth = inputs.shape
    width = requests // local_rows * depth
    query_cols = w_query.shape[1]
    key_cols = w_key.shape[1]
    hidden_cols = w_gate.shape[1]
    rows = requests * steps
    current = inputs.transpose(1, 0, 2).reshape(rows, depth).astype(jnp.float32)
    squares = jnp.sum(current * current, axis=1, keepdims=True)
    scaled = (current * attn_gain).astype(jnp.bfloat16)
    joined = lax.psum_scatter(
        jnp.concatenate(
            [
                jnp.dot(scaled, w_query, preferred_element_type=jnp.float32),
                jnp.dot(scaled, w_key, preferred_element_type=jnp.float32),
                jnp.dot(scaled, w_value, preferred_element_type=jnp.float32),
                jnp.broadcast_to(squares, (rows, 128)),
            ],
            axis=1,
        ),
        "width",
        scatter_dimension=0,
        tiled=True,
    )
    inverse = lax.rsqrt(joined[:, -1:] / width + 1e-05)
    joined = joined * inverse
    shape = (local_rows * steps, -1, HD)
    places = (positions[:, None] + jnp.arange(steps, dtype=jnp.int32)).reshape(-1)
    turned = rotary(joined[:, : query_cols + key_cols].reshape(shape), places).astype(jnp.bfloat16)
    queries = turned[:, : query_cols // HD].reshape(local_rows, steps, -1, HD)
    new_keys = turned[:, query_cols // HD :].reshape(local_rows, steps, -1, HD)
    new_values = joined[:, query_cols + key_cols : query_cols + 2 * key_cols]
    new_values = new_values.astype(jnp.bfloat16).reshape(local_rows, steps, -1, HD)
    mixed = attention(queries, key_cache, value_cache, new_keys, new_values, lengths)
    attn_part = jnp.dot(
        lax.all_gather(mixed.reshape(local_rows * steps, -1), "width", axis=0, tiled=True),
        w_out,
        preferred_element_type=jnp.float32,
    )
    residual = current + lax.psum(attn_part, "hidden")
    res_squares = jnp.sum(residual * residual, axis=1, keepdims=True)
    ffn_in = (residual * ffn_gain).astype(jnp.bfloat16)
    both = lax.psum(
        jnp.concatenate(
            [
                jnp.dot(ffn_in, w_gate, preferred_element_type=jnp.float32),
                jnp.dot(ffn_in, w_up, preferred_element_type=jnp.float32),
                jnp.broadcast_to(res_squares, (rows, 128)),
            ],
            axis=1,
        ),
        "width",
    )
    summed = both * lax.rsqrt(both[:, -1:] / width + 1e-05)
    activated = (
        jax.nn.silu(summed[:, :hidden_cols]) * summed[:, hidden_cols : 2 * hidden_cols]
    ).astype(jnp.bfloat16)
    down_part = jnp.dot(activated, w_down, preferred_element_type=jnp.float32)
    total = lax.psum(down_part, "hidden")
    out = (residual + total).astype(jnp.bfloat16)
    return out.reshape(requests, steps, depth).transpose(1, 0, 2)


MESH = pl.DeviceIdType.MESH
TILE = 512


def far_first(place, n):
    half = n // 2
    flip = lax.div(place, half)
    near = place + flip * (n - 1 - 2 * place)
    alone = n - 1 - 2 * near
    order = []
    for i in range(n - 1):
        j = jnp.maximum(i - alone, 0)
        gap = near - lax.div(j, 2)
        other = jnp.where(i < alone, n - 1 - i, near + gap * (1 - 2 * lax.rem(j, 2)))
        order.append(other + flip * (n - 1 - 2 * other))
    return order


def layer_kernel(
    wide,
    deep,
    lengths_hbm,
    positions_hbm,
    x_hbm,
    attn_gain_hbm,
    ffn_gain_hbm,
    perm_hbm,
    unperm_hbm,
    freqs_hbm,
    w_query,
    w_key,
    w_value,
    w_out,
    w_gate,
    w_up,
    w_down,
    key_cache,
    value_cache,
    out_ref,
    lengths,
    positions,
    x_ref,
    attn_gain,
    ffn_gain,
    perm,
    unperm,
    freqs,
    angle_buf,
    down_buf,
    wq_buf,
    wkv_buf,
    wo_buf,
    wgu_buf,
    kc_buf,
    vc_buf,
    send1,
    recv1,
    ss_send1,
    ss_recv1,
    q_buf,
    k_buf,
    v_buf,
    mix_buf,
    gather,
    out_acc,
    red1,
    res_buf,
    gu_acc,
    send3,
    recv3,
    ss2,
    act_buf,
    red2,
    load_sem,
    small_sem,
    big_sem,
    down_sem,
    s1,
    r1,
    t1,
    u1,
    s2,
    r2,
    s3,
    r3,
    s4,
    r4,
    t4,
    u4,
    s5,
    r5,
    s6,
    r6,
):
    f32, bf16 = jnp.float32, jnp.bfloat16
    col = lax.axis_index("width")
    hid = lax.axis_index("hidden")
    steps, requests, depth = x_ref.shape
    rows = steps * requests
    local_rows, kv_count, slots, _ = kc_buf.shape
    own = steps * local_rows
    query_cols = wq_buf.shape[1]
    key_cols = w_key.shape[1]
    group = query_cols // key_cols
    head_cols = group * HD
    part = act_buf.shape[2]
    pair = 2 * part
    chunks = depth // TILE
    ends, end = red2.shape[1], red2.shape[3]
    width = wide * depth
    far = far_first(col, wide)

    def peer(base, k, n):
        return lax.rem(base + k, n)

    def dot(a, b):
        return jnp.dot(a, b, preferred_element_type=f32)

    sent = []

    def post(src, dst, send_sem, recv_sem, axis, to):
        copy = pltpu.make_async_remote_copy(
            src_ref=src,
            dst_ref=dst,
            send_sem=send_sem,
            recv_sem=recv_sem,
            device_id={axis: to},
            device_id_type=MESH,
        )
        copy.start()
        sent.append(copy)

    def take(dst, send_sem, recv_sem, axis, source):
        pltpu.make_async_remote_copy(
            src_ref=dst,
            dst_ref=dst,
            send_sem=send_sem,
            recv_sem=recv_sem,
            device_id={axis: source},
            device_id_type=MESH,
        ).wait_recv()

    barrier = pltpu.get_barrier_semaphore()
    for k in range(1, wide):
        pl.semaphore_signal(
            barrier, inc=1, device_id={"width": peer(col, k, wide)}, device_id_type=MESH
        )
    for k in range(1, deep):
        pl.semaphore_signal(
            barrier, inc=1, device_id={"hidden": peer(hid, k, deep)}, device_id_type=MESH
        )

    smalls = [
        pltpu.make_async_copy(src, dst, small_sem.at[i])
        for i, (src, dst) in enumerate(
            (
                (x_hbm, x_ref),
                (perm_hbm, perm),
                (attn_gain_hbm, attn_gain),
                (freqs_hbm, freqs),
                (unperm_hbm, unperm),
                (ffn_gain_hbm, ffn_gain),
                (lengths_hbm, lengths),
                (positions_hbm, positions),
            )
        )
    ]
    for load in smalls:
        load.start()
    loads = [
        pltpu.make_async_copy(w_key, wkv_buf.at[0], load_sem.at[0]),
        pltpu.make_async_copy(w_value, wkv_buf.at[1], load_sem.at[1]),
    ]
    pieces = send1.shape[0] - 1
    q_tile = query_cols // pieces
    for c in range(pieces):
        at = pl.ds(c * q_tile, q_tile)
        loads.append(
            pltpu.make_async_copy(w_query.at[:, at], wq_buf.at[:, at], load_sem.at[2 + c])
        )
    key_load = pltpu.make_async_copy(key_cache, kc_buf, load_sem.at[2 + pieces])
    value_load = pltpu.make_async_copy(value_cache, vc_buf, load_sem.at[3 + pieces])
    out_load = pltpu.make_async_copy(w_out, wo_buf, load_sem.at[4 + pieces])
    for load in loads:
        load.start()

    passes = [(0, 1), (1, chunks)] if chunks > 1 else [(0, chunks)]
    slots_of = far + [col]
    big = []
    for n, (lo, hi) in enumerate(passes):
        down = pl.ds(lo * TILE, (hi - lo) * TILE)
        big.append([])
        for i, p in enumerate(slots_of):
            at = pl.ds(pl.multiple_of(p * part, 128), part)
            for m, weight in enumerate((w_gate, w_up)):
                big[n].append(
                    pltpu.make_async_copy(
                        weight.at[down, at],
                        wgu_buf.at[down, pl.ds(i * pair + m * part, part)],
                        big_sem.at[n, i, m],
                    )
                )
    sources = [col] + far[::-1]
    down_loads = []
    for i, p in enumerate(sources):
        at = pl.ds(pl.multiple_of(p * part, 128), part)
        home = wq_buf if i < wide // 2 else wo_buf
        first_row = i % (wide // 2) * part
        down_loads.append(
            (
                pltpu.make_async_copy(
                    w_down.at[at], home.at[pl.ds(first_row, part)], down_sem.at[i]
                ),
                home,
                first_row,
            )
        )

    for load in smalls[:3]:
        load.wait()
    x_bf = jnp.concatenate([x_ref[s].astype(f32) for s in range(steps)], axis=0)
    turned = dot(perm[...], x_bf.astype(bf16))
    squares = jnp.sum(turned * turned, axis=1, keepdims=True)
    squares = jnp.broadcast_to(squares, (rows, 128))
    scaled = (turned * attn_gain[...]).astype(bf16)
    for w in range(wide):
        ss_send1[w] = squares[w * own : (w + 1) * own]

    def put(value, piece):
        value = value.astype(bf16)
        for w in range(wide):
            send1[piece, w] = value[w * own : (w + 1) * own]

    def ship(src, dst, a, b):
        for i, to in enumerate(far):
            post(src.at[to], dst.at[col], a.at[i], b.at[col], "width", to)

    loads[0].wait()
    loads[1].wait()
    put(jnp.concatenate([dot(scaled, wkv_buf[0]), dot(scaled, wkv_buf[1])], axis=1), 0)
    pl.semaphore_wait(barrier, wide + deep - 2)
    ship(ss_send1, ss_recv1, t1, u1)
    ship(send1.at[0], recv1.at[0], s1.at[0], r1.at[0])
    for c in range(pieces):
        loads[2 + c].wait()
        if c == 0:
            key_load.start()
            value_load.start()
        if c == min(1, pieces - 1):
            out_load.start()
        put(dot(scaled, wq_buf[:, c * q_tile : (c + 1) * q_tile]), c + 1)
        ship(send1.at[c + 1], recv1.at[c + 1], s1.at[c + 1], r1.at[c + 1])
        if c == min(2, pieces - 1):
            for load in big[0]:
                load.start()
    for batch in big[1:]:
        for load in batch:
            load.start()
    smalls[3].wait()
    smalls[7].wait()
    for r in range(local_rows):
        for s in range(steps):
            place = (positions[r] + s).astype(f32)
            angle_buf[0, r, s * group : (s + 1) * group, :] = jnp.broadcast_to(
                place * freqs[...], (group, HD)
            )
    lower_half = lax.broadcasted_iota(jnp.int32, (steps * group, HD), 1) < HD // 2
    for r in range(local_rows):
        angle = angle_buf[0, r]
        sin = jnp.sin(angle)
        angle_buf[0, r] = jnp.cos(angle)
        angle_buf[1, r] = jnp.where(lower_half, -sin, sin)

    smalls[6].wait()
    for i, p in enumerate(far):
        take(ss_recv1.at[p], t1.at[i], u1.at[p], "width", p)
    sums = ss_send1[col]
    for p in far:
        sums += ss_recv1[p]
    inverse = lax.rsqrt(sums[:, :1] / width + 1e-05)

    def whole(piece):
        for i, p in enumerate(far):
            take(recv1.at[piece, p], s1.at[piece, i], r1.at[piece, p], "width", p)
        value = send1[piece, col].astype(f32)
        for p in far:
            value += recv1[piece, p].astype(f32)
        return value * inverse

    fresh_kv = whole(0)
    totals = {}
    scale = 1.0 / math.sqrt(HD)
    step_of = lax.broadcasted_iota(jnp.int32, (steps * group, 1), 0)
    slot = lax.broadcasted_iota(jnp.int32, (steps * group, slots), 1)
    for h in range(kv_count):
        needed = range(h * head_cols // q_tile, ((h + 1) * head_cols - 1) // q_tile + 1)
        for piece in needed:
            if piece not in totals:
                totals[piece] = whole(piece + 1)
        for r in range(local_rows):
            for s in range(steps):
                row = r * steps + s
                for g in range(group):
                    at = (h * group + g) * HD
                    line = totals[at // q_tile][row : row + 1]
                    at %= q_tile
                    q_buf[r * kv_count + h, s * group + g : s * group + g + 1, :] = line[
                        :, at : at + HD
                    ]
                line = fresh_kv[row : row + 1]
                at = h * HD
                k_buf[r * kv_count + h, s * group : (s + 1) * group, :] = jnp.broadcast_to(
                    line[:, at : at + HD], (group, HD)
                )
                at += key_cols
                v_buf[r * kv_count + h, s * group : (s + 1) * group, :] = jnp.broadcast_to(
                    line[:, at : at + HD], (group, HD)
                )
        if h == 0:
            key_load.wait()
            value_load.wait()
        asked = []
        for r in range(local_rows):
            cos, sin = angle_buf[0, r], angle_buf[1, r]
            q = q_buf[r * kv_count + h]
            q = (q * cos + pltpu.roll(q, HD // 2, 1) * sin).astype(bf16)
            scores = lax.dot_general(
                q, kc_buf[r, h], (((1,), (1,)), ((), ())), preferred_element_type=f32
            )
            asked.append((q.astype(f32), cos, sin, scores))
        weighed = []
        for r, (q, cos, sin, scores) in enumerate(asked):
            seen = slot < lengths[r]
            nk = k_buf[r * kv_count + h]
            nk = (nk * cos + pltpu.roll(nk, HD // 2, 1) * sin).astype(bf16).astype(f32)
            scores = jnp.where(seen, scores * scale, -1e30)
            highest = jnp.max(scores, axis=1, keepdims=True)
            fresh = []
            for s in range(steps):
                new = jnp.sum(q * nk[s * group : s * group + 1], axis=1, keepdims=True)
                new = jnp.where(step_of >= s * group, new * scale, -1e30)
                fresh.append(new)
                highest = jnp.maximum(highest, new)
            weights = jnp.where(seen, jnp.exp(scores - highest), 0.0)
            for s in range(steps):
                fresh[s] = jnp.where(step_of >= s * group, jnp.exp(fresh[s] - highest), 0.0)
            weighed.append((weights, fresh))
        blends = [
            dot(weights.astype(bf16), vc_buf[r, h]) for r, (weights, _) in enumerate(weighed)
        ]
        for r, (weights, fresh) in enumerate(weighed):
            nv = v_buf[r * kv_count + h].astype(bf16).astype(f32)
            norm = jnp.sum(weights, axis=1, keepdims=True)
            mixed = blends[r]
            for s in range(steps):
                norm += fresh[s]
                mixed += fresh[s].astype(bf16).astype(f32) * nv[s * group : s * group + 1]
            mixed = mixed * (1.0 / norm)
            for s in range(steps):
                row = r * steps + s
                for g in range(group):
                    mix_buf[h, row : row + 1, g * HD : (g + 1) * HD] = mixed[
                        s * group + g : s * group + g + 1
                    ]
        gather[h, col] = mix_buf[h].astype(bf16)
        for i, to in enumerate(far):
            post(gather.at[h, col], gather.at[h, col], s2.at[h, i], r2.at[h, col], "width", to)
    for load in smalls[4:6]:
        load.wait()

    def spread(red, c, a, b):
        for k in range(deep - 1, 0, -1):
            to = peer(hid, k, deep)
            post(red.at[hid, c], red.at[hid, c], a.at[c, k], b.at[c, hid], "hidden", to)

    def reduced(red, c, a, b):
        for k in range(1, deep):
            p = peer(hid, k, deep)
            take(red.at[p, c], a.at[c, k], b.at[c, p], "hidden", p)
        value = red[0, c].astype(f32)
        for i in range(1, deep):
            value += red[i, c].astype(f32)
        return value

    for h in range(kv_count):
        for i, p in enumerate(far[::-1]):
            take(gather.at[h, p], s2.at[h, wide - 2 - i], r2.at[h, p], "width", p)
        mixed = jnp.concatenate([gather[h, w].astype(f32) for w in range(wide)], axis=0)
        mixed = dot(unperm[...], mixed.astype(bf16)).astype(bf16)
        if h == 0:
            out_load.wait()
        for c in range(chunks):
            at = slice(c * TILE, (c + 1) * TILE)
            value = dot(mixed, wo_buf[h * head_cols : (h + 1) * head_cols, at])
            if h:
                value += out_acc[:, at]
            if h < kv_count - 1:
                out_acc[:, at] = value
            else:
                red1[hid, c] = value.astype(bf16)
                spread(red1, c, s3, r3)
    for load, _, _ in down_loads:
        load.start()

    res_squares = jnp.zeros((rows, 1), f32)
    for n, (lo, hi) in enumerate(passes):
        for c in range(lo, hi):
            at = slice(c * TILE, (c + 1) * TILE)
            value = reduced(red1, c, s3, r3)
            value += jnp.concatenate([x_ref[s, :, at].astype(f32) for s in range(steps)], axis=0)
            res_buf[:, at] = value
            res_squares += jnp.sum(value * value, axis=1, keepdims=True)
        last = n == len(passes) - 1
        if last:
            ss2[col] = jnp.broadcast_to(res_squares, (rows, 128))
            for i, to in enumerate(far):
                post(ss2.at[col], ss2.at[col], t4.at[i], u4.at[col], "width", to)
        deep_at = slice(lo * TILE, hi * TILE)
        ffn_in = (res_buf[:, deep_at] * ffn_gain[:, deep_at]).astype(bf16)
        for load in big[n]:
            load.wait()
        shipped = 0
        for c in range(wide * pair // TILE):
            at = slice(c * TILE, (c + 1) * TILE)
            value = dot(ffn_in, wgu_buf[deep_at, at])
            if n:
                value += gu_acc[:, at]
            if not last:
                gu_acc[:, at] = value
                continue
            send3[:, at] = value.astype(bf16)
            while shipped < 2 * (wide - 1) and (shipped + 1) * part <= (c + 1) * TILE:
                i, m = shipped // 2, shipped % 2
                mine = send3.at[:, pl.ds(shipped * part, part)]
                post(mine, recv3.at[col, m], s4.at[i, m], r4.at[col, m], "width", far[i])
                shipped += 1
    at = (wide - 1) * pair
    gate = send3[:, at : at + part].astype(f32)
    up = send3[:, at + part : at + pair].astype(f32)
    sums = ss2[col]
    for i, p in enumerate(far):
        take(ss2.at[p], t4.at[i], u4.at[p], "width", p)
        sums += ss2[p]
    inverse = lax.rsqrt(sums[:, :1] / width + 1e-05)
    for i, p in enumerate(far):
        for m in range(2):
            take(recv3.at[p, m], s4.at[i, m], r4.at[p, m], "width", p)
    for p in far:
        gate += recv3[p, 0].astype(f32)
        up += recv3[p, 1].astype(f32)
    gate, up = gate * inverse, up * inverse
    act_buf[col] = (gate / (1.0 + jnp.exp(-gate)) * up).astype(bf16)
    for i, to in enumerate(far):
        post(act_buf.at[col], act_buf.at[col], s5.at[i], r5.at[col], "width", to)
    for i, p in enumerate(sources):
        if i:
            take(act_buf.at[p], s5.at[wide - 1 - i], r5.at[p], "width", p)
        load, home, first_row = down_loads[i]
        load.wait()
        act = act_buf[p]
        for c in range(ends):
            at = slice(c * end, (c + 1) * end)
            value = dot(act, home[first_row : first_row + part, at])
            if i:
                value += down_buf[:, at]
            if i < wide - 1:
                down_buf[:, at] = value
            else:
                red2[hid, c] = value.astype(bf16)
                spread(red2, c, s6, r6)
    for c in range(ends):
        at = slice(c * end, (c + 1) * end)
        value = res_buf[:, at] + reduced(red2, c, s6, r6)
        for s in range(steps):
            out_ref[s, :, at] = value[s * requests : (s + 1) * requests]
    for copy in sent:
        copy.wait_send()


def fused(
    wide,
    deep,
    inputs,
    attn_gain,
    w_query,
    w_key,
    w_value,
    w_out,
    ffn_gain,
    w_gate,
    w_up,
    w_down,
    key_cache,
    value_cache,
    lengths,
    positions,
):
    steps, requests, depth = inputs.shape
    rows = steps * requests
    local_rows, kv_count, slots, _ = key_cache.shape
    own = steps * local_rows
    query_cols, key_cols = w_query.shape[1], w_key.shape[1]
    group = query_cols // key_cols
    part = w_gate.shape[1] // wide
    chunks = depth // TILE
    ends = max(1, chunks // 2)
    source = np.arange(rows).reshape(steps, wide, local_rows).transpose(1, 2, 0).reshape(-1)
    perm = np.zeros((rows, rows), np.float32)
    perm[np.arange(rows), source] = 1.0
    half_dim = HD // 2
    freqs = 500000.0 ** (-(np.arange(half_dim) * 2.0 / HD))
    freqs = jnp.asarray(np.concatenate([freqs, freqs])[None], jnp.float32)
    pieces = query_cols // (2 * key_cols)
    hbm = pl.BlockSpec(memory_space=pl.ANY)
    bf16, f32 = jnp.bfloat16, jnp.float32
    dma = pltpu.SemaphoreType.DMA
    heads = local_rows * kv_count
    scratch = [
        pltpu.SMEM(lengths.shape, jnp.int32),
        pltpu.SMEM(positions.shape, jnp.int32),
        pltpu.VMEM(inputs.shape, bf16),
        pltpu.VMEM((1, depth), f32),
        pltpu.VMEM((1, depth), f32),
        pltpu.VMEM((rows, rows), bf16),
        pltpu.VMEM((rows, rows), bf16),
        pltpu.VMEM((1, HD), f32),
        pltpu.VMEM((2, local_rows, steps * group, HD), f32),
        pltpu.VMEM((rows, depth), f32),
        pltpu.VMEM((depth, query_cols), bf16),
        pltpu.VMEM((2, depth, key_cols), bf16),
        pltpu.VMEM((query_cols, depth), bf16),
        pltpu.VMEM((depth, wide * 2 * part), bf16),
        pltpu.VMEM(key_cache.shape, bf16),
        pltpu.VMEM(value_cache.shape, bf16),
        pltpu.VMEM((pieces + 1, wide, own, 2 * key_cols), bf16),
        pltpu.VMEM((pieces + 1, wide, own, 2 * key_cols), bf16),
        pltpu.VMEM((wide, own, 128), f32),
        pltpu.VMEM((wide, own, 128), f32),
        pltpu.VMEM((heads, steps * group, HD), f32),
        pltpu.VMEM((heads, steps * group, HD), f32),
        pltpu.VMEM((heads, steps * group, HD), f32),
        pltpu.VMEM((kv_count, own, group * HD), f32),
        pltpu.VMEM((kv_count, wide, own, group * HD), bf16),
        pltpu.VMEM((rows, depth), f32),
        pltpu.VMEM((deep, chunks, rows, TILE), bf16),
        pltpu.VMEM((rows, depth), f32),
        pltpu.VMEM((rows, wide * 2 * part), f32),
        pltpu.VMEM((rows, wide * 2 * part), bf16),
        pltpu.VMEM((wide, 2, rows, part), bf16),
        pltpu.VMEM((wide, rows, 128), f32),
        pltpu.VMEM((wide, rows, part), bf16),
        pltpu.VMEM((deep, ends, rows, depth // ends), bf16),
        dma((pieces + 5,)),
        dma((8,)),
        dma((2, wide, 2)),
        dma((wide,)),
        dma((pieces + 1, wide)),
        dma((pieces + 1, wide)),
        dma((wide,)),
        dma((wide,)),
        dma((kv_count, wide)),
        dma((kv_count, wide)),
        dma((chunks, deep)),
        dma((chunks, deep)),
        dma((wide, 2)),
        dma((wide, 2)),
        dma((wide,)),
        dma((wide,)),
        dma((wide,)),
        dma((wide,)),
        dma((ends, deep)),
        dma((ends, deep)),
    ]
    return pl.pallas_call(
        functools.partial(layer_kernel, wide, deep),
        out_shape=pltpu.VMEM(inputs.shape, f32),
        in_specs=[hbm] * 17,
        out_specs=pl.BlockSpec(memory_space=pltpu.VMEM),
        scratch_shapes=scratch,
        compiler_params=pltpu.CompilerParams(
            collective_id=0, has_side_effects=True, vmem_limit_bytes=56 * 1024 * 1024
        ),
        name="layer",
    )(
        lengths,
        positions,
        inputs,
        attn_gain[None],
        ffn_gain[None],
        jnp.asarray(perm, bf16),
        jnp.asarray(perm.T, bf16),
        freqs,
        w_query,
        w_key,
        w_value,
        w_out,
        w_gate,
        w_up,
        w_down,
        key_cache,
        value_cache,
    ).astype(bf16)


def local(wide, deep, *arrays):
    inputs, w_query, w_gate = arrays[0], arrays[2], arrays[7]
    fits = (
        wide % 2 == 0
        and wide <= 8
        and inputs.shape[1] % 8 == 0
        and inputs.shape[0] * inputs.shape[1] <= 32
        and w_query.shape[1] == w_query.shape[0]
        and w_query.shape[1] % (2 * arrays[3].shape[1]) == 0
        and w_gate.shape[1] // 2 <= w_query.shape[0]
        and w_gate.shape[1] % (wide * 128) == 0
        and w_gate.shape[1] * 2 % TILE == 0
        and w_query.shape[0] % (2 * TILE) == 0
    )
    return fused(wide, deep, *arrays) if fits else plain(*arrays)


def solution(mesh):
    in_specs = (
        P(None, "groups", "width"),
        P("width"),
        P("width", "hidden"),
        P("width", "hidden"),
        P("width", "hidden"),
        P("hidden", "width"),
        P("width"),
        P("width", "hidden"),
        P("width", "hidden"),
        P("hidden", "width"),
        P(("groups", "width"), "hidden", None, None),
        P(("groups", "width"), "hidden", None, None),
        P(("groups", "width")),
        P(("groups", "width")),
    )
    out_specs = P(None, "groups", "width")
    step = functools.partial(local, mesh.shape["width"], mesh.shape["hidden"])
    return jax.shard_map(step, mesh=mesh, in_specs=in_specs, out_specs=out_specs, check_vma=False)
```
